768 devices in a mesh: rows: 64 (over y, z_hi, core), rep: 12 (over z_lo, x).
Axes of the slice: x: 4, y: 8, z: 12 (z_hi: 4, z_lo: 3; z = z_hi * 3 + z_lo), core: 2. Of those that a mesh axis runs over, the one named last changes fastest.
Arguments:
- features: bfloat16 [98304, 256], P(('rows', 'rep')), may hold values from -6 to 6
- weight: bfloat16 [256, 256], replicated, may hold values from -0.375 to 0.375
- tiles: bfloat16 [64, 12, 12, 8, 128, 128], P('rows', 'rep'), as said below
- send_src: int32 [64, 12, 64, 24], P('rows', 'rep'), may hold values from 0 to 12287, as said below
- send_dst: int32 [64, 12, 64, 24], P('rows', 'rep'), may hold values from 0 to 128, as said below
- cotangent: bfloat16 [98304, 256], P(('rows', 'rep')), may hold values from -6 to 6
Outputs:
- output: bfloat16 [98304, 256], P(('rows', 'rep'))
- grad_w: float32 [256, 256], replicated
- grad_x: bfloat16 [98304, 256], P(('rows', 'rep'))
The draws below stay inside these ranges and needn't reach their ends.
Inputs may be any that keep to these rules, and one draw needn't show every extreme that they name: Device (g, c)'s tiles are nonnegative; a tile row is nonzero only if some live slot of that device names it. `send_src`: A flattened tile row (b * 8 + k) * 128 + i of the sending device. Each tile row is named by at most one live slot, and all live slots naming rows of one tile belong to one peer p. An empty slot holds 0. `send_dst`: 128 marks an empty slot. For each rep index c there is a peer p to which every device (g, c) sends all 24 slots live, and some device has an empty slot. Destination rows may repeat.
All inputs are finite; a program needn't handle non-finite values.
Results may differ from the reference program's by a relative error of at most 0.02.
Values may be sent and summed in bfloat16 or wider, within the bound.
A program may use at most 64 MiB of HBM per device.

```python
import math
import jax
import jax.numpy as jnp
from jax import lax

F = 256
BLK = 128
ROWS_DEV = 128
KPC = 8
SLOTS = 24
GROUPS = 64
REPS = 12
CBLK = 12
NODES = 98304


def layout(key):
    base_key = jax.random.fold_in(key, 11)
    sub_keys = jax.random.split(base_key, 10)
    device_count = GROUPS * REPS
    tile_count = CBLK * KPC
    column_peer = jax.random.randint(sub_keys[0], (REPS,), 0, GROUPS)
    full_peer = jnp.tile(column_peer, GROUPS)
    first_draw = jax.random.randint(sub_keys[1], (device_count, tile_count), 0, GROUPS)
    second_draw = jax.random.randint(sub_keys[2], (device_count, tile_count), 0, GROUPS)
    offsets = jax.random.randint(sub_keys[3], (device_count, 1), 0, GROUPS)
    peers = (first_draw * second_draw // GROUPS + offsets) % GROUPS
    special = jax.random.randint(sub_keys[4], (device_count, 1), 0, tile_count)
    tile_index = jnp.arange(tile_count, dtype=jnp.int32)
    peers = jnp.where(tile_index[None, :] == special, full_peer[:, None], peers)
    matching = peers[:, :, None] == peers[:, None, :]
    earlier = tile_index[None, None, :] < tile_index[None, :, None]
    ranks = jnp.sum(matching & earlier, axis=2).astype(jnp.int32)
    peer_index = jnp.arange(GROUPS, dtype=jnp.int32)
    owned = peers[:, None, :] == peer_index[None, :, None]
    tally = jnp.sum(owned, axis=2).astype(jnp.int32)
    slot_index = jnp.arange(SLOTS, dtype=jnp.int32)
    divisor = jnp.maximum(tally, 1)[:, :, None]
    want_rank = slot_index[None, None, :] % divisor
    depth = slot_index[None, None, :] // divisor
    chosen = owned[:, :, None, :] & (ranks[:, None, None, :] == want_rank[:, :, :, None])
    tile_pick = jnp.sum(jnp.where(chosen, tile_index, 0), axis=3).astype(jnp.int32)
    row_start = jax.random.randint(sub_keys[5], (device_count, tile_count), 0, BLK)
    row_step = 2 * jax.random.randint(sub_keys[6], (device_count, tile_count), 0, BLK // 2) + 1
    flat_pick = tile_pick.reshape(device_count, GROUPS * SLOTS)
    start_sel = jnp.take_along_axis(row_start, flat_pick, axis=1).reshape(device_count, GROUPS, SLOTS)
    step_sel = jnp.take_along_axis(row_step, flat_pick, axis=1).reshape(device_count, GROUPS, SLOTS)
    row_pick = (start_sel + depth * step_sel) % BLK
    keeping = jax.random.randint(sub_keys[7], (device_count, GROUPS, SLOTS), 0, 8) > 0
    is_full = peer_index[None, :, None] == full_peer[:, None, None]
    live = (tally[:, :, None] > 0) & (keeping | is_full)
    blank_device = jax.random.randint(sub_keys[8], (), 0, device_count)
    device_index = jnp.arange(device_count, dtype=jnp.int32)
    blank_peer = (full_peer[:, None, None] + 1) % GROUPS
    blank = (device_index[:, None, None] == blank_device) & (peer_index[None, :, None] == blank_peer) & (slot_index[None, None, :] == SLOTS - 1)
    live = live & jnp.logical_not(blank)
    sources = jnp.where(live, tile_pick * BLK + row_pick, 0).astype(jnp.int32)
    landing_rows = jax.random.randint(sub_keys[9], (device_count, GROUPS, SLOTS), 0, ROWS_DEV)
    targets = jnp.where(live, landing_rows, ROWS_DEV).astype(jnp.int32)
    return (live, sources, targets)


def draw_send_src(key, part):
    live, sources, targets = layout(key)
    return sources.reshape(GROUPS, REPS, GROUPS, SLOTS)


def draw_send_dst(key, part):
    live, sources, targets = layout(key)
    return targets.reshape(GROUPS, REPS, GROUPS, SLOTS)


def draw_tiles(key, part):
    live, sources, targets = layout(key)
    device_count = GROUPS * REPS
    tile_count = CBLK * KPC
    device_index = jnp.broadcast_to(jnp.arange(device_count, dtype=jnp.int32)[:, None, None], sources.shape)
    marks = jnp.zeros((device_count, tile_count * BLK), jnp.float32)
    marks = marks.at[device_index, sources].max(live.astype(jnp.float32))
    value_key = jax.random.fold_in(key, 29)
    shape = (device_count, tile_count, BLK, BLK)
    values = jnp.exp(jax.random.uniform(value_key, shape, jnp.float32, math.log(0.05), 0.0))
    values = values * (1.5 / math.sqrt(BLK)) * marks.reshape(device_count, tile_count, BLK, 1)
    return values.reshape(GROUPS, REPS, CBLK, KPC, BLK, BLK).astype(jnp.bfloat16)


def level_of(rng, dims, pieces, least, largest):
    def one(axis_at, blocks):
        steps = jax.random.uniform(jax.random.fold_in(jax.random.fold_in(rng, 6), axis_at), (blocks,), jnp.float32, least / len(pieces), largest / len(pieces))
        return jnp.repeat(jnp.exp(steps), dims[axis_at] // blocks).reshape((-1,) + (1,) * (len(dims) - axis_at - 1))

    level = one(*pieces[0])
    for cut in pieces[1:]:
        level = level * one(*cut)
    return level


def scatter_about(own_key, shape, scale, most, shards=(), held_as=jnp.bfloat16):
    entries = scale * jax.random.normal(own_key, shape, jnp.float32)
    if shards:
        entries = entries * level_of(own_key, shape, shards, -0.22, 0.18)
    return jnp.clip(entries, -most, most).astype(held_as)


def setup_inputs(seed: int = 0) -> dict:
    streams_of = jax.random.split(jax.random.key(seed), 7)
    features = scatter_about(streams_of[0], (NODES, F), 1.0, 6.0, ((0, 768),))
    weight = scatter_about(streams_of[1], (F, F), F ** -0.5, 0.375)
    tiles = draw_tiles(jax.random.fold_in(streams_of[6], 71), 0)
    send_src = draw_send_src(jax.random.fold_in(streams_of[6], 71), 0)
    send_dst = draw_send_dst(jax.random.fold_in(streams_of[6], 71), 0)
    cotangent = scatter_about(streams_of[5], (NODES, F), 1.0, 6.0, ((0, 768),))
    return dict(features=features, weight=weight, tiles=tiles, send_src=send_src, send_dst=send_dst, cotangent=cotangent)


def pick_rows(partial_rows, row_index):
    return partial_rows[row_index]

def place_rows(row_index, row_values, tile_rows, feature_width):
    return jnp.zeros((tile_rows, feature_width), jnp.float32).at[row_index].set(row_values.astype(jnp.float32), mode='drop')

def reference(features, weight, tiles, send_src, send_dst, cotangent):
    feature_width = features.shape[1]
    group_size = REPS * ROWS_DEV
    tile_rows = CBLK * KPC * BLK
    grouped = features.reshape(GROUPS, CBLK, BLK, feature_width)
    rep_index = jnp.arange(REPS, dtype=jnp.int32)
    peer_index = jnp.arange(GROUPS, dtype=jnp.int32)
    group_list = jnp.arange(GROUPS, dtype=jnp.int32)

    def destinations(group_dst):
        base_row = (peer_index[None, :, None] * REPS + rep_index[:, None, None]) * ROWS_DEV
        return jnp.where(group_dst < ROWS_DEV, base_row + group_dst, NODES).astype(jnp.int32)

    def forward_group(running, group_index):
        feature_blocks = grouped[group_index].astype(jnp.float32)
        tile_group = tiles[group_index].astype(jnp.float32)
        partial_value = jnp.einsum('cbkij,bjf->cbkif', tile_group, feature_blocks).reshape(REPS, tile_rows, feature_width)
        sources = send_src[group_index].reshape(REPS, GROUPS * SLOTS)
        fetched = jax.vmap(pick_rows)(partial_value, sources)
        landing = destinations(send_dst[group_index]).reshape(-1)
        running = running.at[landing].add(fetched.reshape(-1, feature_width), mode='drop')
        return (running, None)
    gathered, _ = lax.scan(forward_group, jnp.zeros((NODES, feature_width), jnp.float32), group_list)
    aggregated = (features.astype(jnp.float32) + gathered).astype(jnp.bfloat16)
    preact = jnp.dot(aggregated, weight, preferred_element_type=jnp.float32)
    sigmoid = jax.nn.sigmoid(preact)
    output = (preact * sigmoid).astype(jnp.bfloat16)
    pre_grad = (cotangent.astype(jnp.float32) * sigmoid * (1.0 + preact * (1.0 - sigmoid))).astype(jnp.bfloat16)
    grad_w = jnp.dot(aggregated.T, pre_grad, preferred_element_type=jnp.float32) * (1.0 / math.sqrt(NODES))
    back_in = jnp.dot(pre_grad, weight.T, preferred_element_type=jnp.float32).astype(jnp.bfloat16)

    def backward_group(group_index):
        landing = destinations(send_dst[group_index])
        fetched = back_in[jnp.minimum(landing, NODES - 1)]
        keep_source = jnp.where(send_dst[group_index] < ROWS_DEV, send_src[group_index], tile_rows).astype(jnp.int32)
        spread = jax.vmap(place_rows, in_axes=(0, 0, None, None))(keep_source.reshape(REPS, -1), fetched.reshape(REPS, -1, feature_width), tile_rows, feature_width)
        spread = spread.reshape(REPS, CBLK, KPC, BLK, feature_width)
        tile_group = tiles[group_index].astype(jnp.float32)
        return jnp.einsum('cbkij,cbkif->bjf', tile_group, spread).reshape(group_size, feature_width)
    column_terms = lax.map(backward_group, group_list)
    grad_x = (back_in.astype(jnp.float32) + column_terms.reshape(NODES, feature_width)).astype(jnp.bfloat16)
    return (output, grad_w, grad_x)
```

```python
import math

import jax
import jax.numpy as jnp
from jax import lax
from jax.experimental import pallas as pl
from jax.experimental.pallas import tpu as pltpu
from jax.sharding import PartitionSpec as P

MESH = pl.DeviceIdType.MESH
BF = jnp.bfloat16
F32 = jnp.float32

NY, ZH, NC, ZL, NX = 8, 4, 2, 3, 4
NJ = NY * NC
NREP = ZL * NX
NM = NC * NX
NZ = ZH * ZL
SLOT = 24
MSG = ZH * SLOT
BLK = 128
F = 256
PER_COL = 8
NCOL = 12
NODES = 98304


def _copy(src, dst, ssem, rsem, rows, rep):
    return pltpu.make_async_remote_copy(
        src_ref=src,
        dst_ref=dst,
        send_sem=ssem,
        recv_sem=rsem,
        device_id=(rows, rep),
        device_id_type=MESH,
    )


def _kernel(
    feat, weight, cot, tiles, src, bid, key,
    out, gw, gx,
    X, tb, tf, G, A, AT, keys, U, s1, r1, acc, s2, r2, BI, s3, R, ts, town, rs,
    W, WA, w1, WB, WC, WD, WE,
    loc_sem, ag_s, ag_r, k_s, k_r, y1_s, y1_r, z1_s, z1_r, z2_s, z2_r, y2_s, y2_r,
    rs_s, rs_r, a_s, a_r, b_s, b_r, c_s, c_r, d_s, d_r, e_s, e_r,
):
    r = lax.axis_index("rows")
    c = lax.axis_index("rep")
    y, zh, core = r // (ZH * NC), (r // NC) % ZH, r % NC
    zl, x = c // NX, c % NX
    j = y * NC + core
    m = core * NX + x
    z = zh * ZL + zl

    def row_of(yy, hh, cc):
        return (yy * ZH + hh) * NC + cc

    def plane(jj):
        return row_of(jj // NC, zh, jj % NC), c

    def column(hh):
        return row_of(y, hh, core), c

    def pair(mm):
        return row_of(y, zh, mm // NX), zl * NX + mm % NX

    def along_y(yy):
        return row_of(yy, zh, core), c

    def along_z(zz):
        return row_of(y, zz // ZL, core), (zz % ZL) * NX + x

    def each(count, me, fn):
        def step(k, carry):
            fn((me + k) % count)
            return carry

        lax.fori_loop(1, count, step, 0)

    def ag(cc, own):
        return _copy(feat, X.at[own], ag_s.at[cc], ag_r.at[own], r, cc)

    def kx(jj, own):
        return _copy(key.at[jj], keys.at[own], k_s.at[jj], k_r.at[own], *plane(jj))

    def y1(jj, own):
        return _copy(s1.at[jj], r1.at[own, pl.ds(0, MSG)], y1_s.at[jj], y1_r.at[own], *plane(jj))

    def z1(hh, own):
        return _copy(s2.at[hh], r2.at[own], z1_s.at[hh], z1_r.at[own], *column(hh))

    def z2(hh, own):
        return _copy(BI.at[zh], BI.at[own], z2_s.at[hh], z2_r.at[own], *column(hh))

    def y2(jj, own):
        return _copy(s3.at[jj], R.at[own, pl.ds(0, MSG)], y2_s.at[jj], y2_r.at[own], *plane(jj))

    def rx(cc, own):
        return _copy(ts.at[cc], rs.at[own], rs_s.at[cc], rs_r.at[own], r, cc)

    def ga(mm, own):
        return _copy(W.at[mm], WA.at[own], a_s.at[mm], a_r.at[own], *pair(mm))

    def gb(yy, own):
        return _copy(w1.at[yy], WB.at[own], b_s.at[yy], b_r.at[own], *along_y(yy))

    def gc(zz, own):
        return _copy(WC.at[z], WC.at[own], c_s.at[zz], c_r.at[own], *along_z(zz))

    def gd(yy, own):
        return _copy(WD.at[y], WD.at[own], d_s.at[yy], d_r.at[own], *along_y(yy))

    def ge(mm, own):
        return _copy(WE.at[m], WE.at[own], e_s.at[mm], e_r.at[own], *pair(mm))

    def start(make, count, me):
        each(count, me, lambda o: make(o, me).start())

    def arrive(make, count, me):
        each(count, me, lambda o: make(o, o).wait_recv())

    def sent(make, count, me):
        each(count, me, lambda o: make(o, me).wait_send())

    load = pltpu.make_async_copy(tiles, tb, loc_sem)
    load.start()

    barrier = pltpu.get_barrier_semaphore()

    def greet(rows, rep):
        pl.semaphore_signal(barrier, inc=1, device_id=(rows, rep), device_id_type=MESH)

    each(NREP, c, lambda cc: greet(r, cc))
    each(NJ, j, lambda jj: greet(*plane(jj)))
    each(ZH, zh, lambda hh: greet(*column(hh)))
    each(NX, x, lambda xx: greet(row_of(y, zh, 1 - core), zl * NX + xx))
    each(ZH, zh, lambda hh: each(ZL, zl, lambda ll: greet(row_of(y, hh, core), ll * NX + x)))
    pl.semaphore_wait(barrier, (NREP - 1) + (NJ - 1) + (ZH - 1) + (NX - 1) + (ZH - 1) * (ZL - 1))

    start(ag, NREP, c)
    start(kx, NJ, j)
    X[c] = feat[...]
    keys[j] = key[j]

    def clear(jj, carry):
        r1[jj, MSG:BLK, :] = jnp.zeros((BLK - MSG, F), BF)
        R[jj, MSG:BLK, :] = jnp.zeros((BLK - MSG, F), BF)
        return carry

    lax.fori_loop(0, NJ, clear, 0)

    load.wait()

    def widen(t, carry):
        at = pl.multiple_of(t * BLK, BLK)
        tf[pl.ds(at, BLK), :] = tb[pl.ds(at, BLK), :].astype(F32)
        return carry

    lax.fori_loop(0, NCOL * PER_COL, widen, 0)

    def column_of(row):
        return jnp.transpose(jnp.broadcast_to(row, (BLK, BLK)))

    def gather(jj, carry):
        for i in range(MSG):
            G[jj, i : i + 1, :] = tf[pl.ds(src[jj, i], 1), :]
        rows = G[jj, 0:MSG, :]
        where = column_of(bid[jj].astype(F32))[0:MSG, :]
        for b in range(NCOL):
            A[jj, :, b * BLK : (b + 1) * BLK] = jnp.where(where == b, rows, 0.0).astype(BF)
        return carry

    lax.fori_loop(0, NJ, gather, 0)

    arrive(ag, NREP, c)

    for t in range(NJ // 4):
        at = ((j // 4 + t) % 4) * 4
        rows = jnp.dot(
            A[pl.ds(at, 4)].reshape(4 * MSG, NCOL * BLK),
            X[...].reshape(NREP * BLK, F),
            preferred_element_type=F32,
        )
        s1[pl.ds(at, 4)] = rows.reshape(4, MSG, F).astype(BF)
        for u in range(4):
            jj = at + (j + u) % 4

            @pl.when(jj != j)
            def _():
                y1(jj, j).start()

    r1[j, 0:MSG, :] = s1[j]

    arrive(kx, NJ, j)
    lanes = lax.broadcasted_iota(jnp.int32, (MSG, BLK), 1).astype(F32)

    def mirror(jj, carry):
        where = column_of(keys[jj].astype(F32))[0:MSG, :]
        for h in range(ZH):
            U[jj, :, h * BLK : (h + 1) * BLK] = jnp.where(
                where == lanes + float(h * BLK), 1.0, 0.0
            ).astype(BF)
        turned = jnp.transpose(G[jj])
        row = bid[jj].astype(F32)
        at = pl.multiple_of(jj * BLK, BLK)
        for b in range(NCOL):
            AT[b, :, pl.ds(at, BLK)] = jnp.where(row == b, turned, 0.0).astype(BF)
        return carry

    lax.fori_loop(0, NJ, mirror, 0)

    heads = lax.broadcasted_iota(jnp.int32, (ZH * BLK, BLK), 0)

    def picked(jj):
        hot = jnp.where(keys[jj] == heads, 1.0, 0.0).astype(BF)
        return jnp.dot(hot, r1[jj], preferred_element_type=F32).reshape(ZH, BLK, F)

    acc[...] = picked(j)

    def add_rows(k, carry):
        jj = (j + k) % NJ
        y1(jj, jj).wait_recv()
        acc[...] += picked(jj)
        return carry

    lax.fori_loop(1, NJ, add_rows, 0)

    for k in range(1, ZH):
        hh = (zh + k) % ZH
        s2[hh] = acc[hh].astype(BF)
        z1(hh, zh).start()
    summed = feat[...].astype(F32) + acc[zh]
    arrive(z1, ZH, zh)
    for k in range(1, ZH):
        summed += r2[(zh + k) % ZH].astype(F32)
    aggregated = summed.astype(BF)

    preact = jnp.dot(aggregated, weight[...], preferred_element_type=F32)
    sigmoid = jax.nn.sigmoid(preact)
    pre_grad = (cot[...].astype(F32) * sigmoid * (1.0 + preact * (1.0 - sigmoid))).astype(BF)
    back_in = lax.dot_general(
        pre_grad, weight[...], (((1,), (1,)), ((), ())), preferred_element_type=F32
    ).astype(BF)
    BI[zh] = back_in
    start(z2, ZH, zh)

    out[...] = (preact * sigmoid).astype(BF)
    local_w = lax.dot_general(
        aggregated, pre_grad, (((0,), (0,)), ((), ())), preferred_element_type=F32
    )
    W[0 : NM // 2] = local_w[:, 0:BLK].reshape(NM // 2, NY, 8, BLK)
    W[NM // 2 : NM] = local_w[:, BLK:F].reshape(NM // 2, NY, 8, BLK)
    start(ga, NM, m)

    arrive(z2, ZH, zh)
    for t in range(NJ // 4):
        at = ((j // 4 + t) % 4) * 4
        rows = jnp.dot(
            U[pl.ds(at, 4)].reshape(4 * MSG, ZH * BLK),
            BI[...].reshape(ZH * BLK, F),
            preferred_element_type=F32,
        )
        s3[pl.ds(at, 4)] = rows.reshape(4, MSG, F).astype(BF)
        for u in range(4):
            jj = at + (j + u) % 4

            @pl.when(jj != j)
            def _():
                y2(jj, j).start()

    R[j, 0:MSG, :] = s3[j]

    arrive(ga, NM, m)
    total = W[m]
    for k in range(1, NM):
        total += WA[(m + k) % NM]
    w1[...] = total
    start(gb, NY, y)
    arrive(gb, NY, y)
    total = w1[y]
    for k in range(1, NY):
        total += WB[(y + k) % NY]
    WC[z] = total
    start(gc, NZ, z)
    arrive(gc, NZ, z)
    total = WC[0]
    for k in range(1, NZ):
        total += WC[k]
    WD[y] = total * (1.0 / math.sqrt(NODES))
    start(gd, NY, y)
    arrive(gd, NY, y)
    WE[m] = WD[...]
    start(ge, NM, m)

    arrive(y2, NJ, j)
    for t in range(ZL):
        at = ((zl + t) % ZL) * NX
        terms = jnp.dot(
            AT[pl.ds(at, NX)].reshape(NX * BLK, NJ * BLK),
            R[...].reshape(NJ * BLK, F),
            preferred_element_type=F32,
        ).reshape(NX, BLK, F)
        ts[pl.ds(at, NX)] = terms.astype(BF)
        if t == 0:
            town[...] = terms
        for u in range(NX):
            cc = at + (x + u) % NX

            @pl.when(cc != c)
            def _():
                rx(cc, c).start()

    arrive(ge, NM, m)
    for half in range(2):
        gw[:, half * BLK : (half + 1) * BLK] = WE[half * NM // 2 : (half + 1) * NM // 2].reshape(
            F, BLK
        )

    result = BI[zh].astype(F32) + town[x]
    arrive(rx, NREP, c)
    for k in range(1, NREP):
        result += rs[(c + k) % NREP].astype(F32)
    gx[...] = result.astype(BF)

    for make, count, me in (
        (ag, NREP, c), (kx, NJ, j), (y1, NJ, j), (z1, ZH, zh), (z2, ZH, zh), (y2, NJ, j),
        (rx, NREP, c), (ga, NM, m), (gb, NY, y), (gc, NZ, z), (gd, NY, y), (ge, NM, m),
    ):
        sent(make, count, me)


def local(features, weight, tiles, send_src, send_dst, cotangent):
    def ordered(a):
        return a.reshape(NY, ZH, NC, SLOT).transpose(0, 2, 1, 3).reshape(NJ, MSG)

    source = ordered(send_src[0, 0])
    target = ordered(send_dst[0, 0])
    step = jnp.repeat(jnp.arange(ZH, dtype=jnp.int32) * BLK, SLOT)[None, :]
    pad = ((0, 0), (0, BLK - MSG))
    key = jnp.where(target < BLK, target + step, -1)
    key = jnp.pad(key, pad, constant_values=-1).reshape(NJ, 1, BLK)
    bid = jnp.pad(source // (PER_COL * BLK), pad, constant_values=-1).reshape(NJ, 1, BLK)
    V = pltpu.VMEM
    dma = pltpu.SemaphoreType.DMA
    vmem = pl.BlockSpec(memory_space=pltpu.VMEM)
    rows = NCOL * PER_COL * BLK
    return pl.pallas_call(
        _kernel,
        out_shape=(
            jax.ShapeDtypeStruct((BLK, F), BF),
            jax.ShapeDtypeStruct((F, F), F32),
            jax.ShapeDtypeStruct((BLK, F), BF),
        ),
        in_specs=[
            vmem, vmem, vmem, pl.BlockSpec(memory_space=pl.ANY),
            pl.BlockSpec(memory_space=pltpu.SMEM), vmem, vmem,
        ],
        out_specs=(vmem, vmem, vmem),
        scratch_shapes=[
            V((NREP, BLK, F), BF),
            V((rows, BLK), BF),
            V((rows, BLK), F32),
            V((NJ, BLK, BLK), F32),
            V((NJ, MSG, NCOL * BLK), BF),
            V((NCOL, BLK, NJ * BLK), BF),
            V((NJ, 1, BLK), jnp.int32),
            V((NJ, MSG, ZH * BLK), BF),
            V((NJ, MSG, F), BF),
            V((NJ, BLK, F), BF),
            V((ZH, BLK, F), F32),
            V((ZH, BLK, F), BF),
            V((ZH, BLK, F), BF),
            V((ZH, BLK, F), BF),
            V((NJ, MSG, F), BF),
            V((NJ, BLK, F), BF),
            V((NREP, BLK, F), BF),
            V((NX, BLK, F), F32),
            V((NREP, BLK, F), BF),
            V((NM, NY, 8, BLK), F32),
            V((NM, NY, 8, BLK), F32),
            V((NY, 8, BLK), F32),
            V((NY, 8, BLK), F32),
            V((NZ, 8, BLK), F32),
            V((NY, 8, BLK), F32),
            V((NM, NY, 8, BLK), F32),
            dma,
            *[dma((n,)) for n in (NREP, NJ, NJ, ZH, ZH, NJ, NREP, NM, NY, NZ, NY, NM) for _ in range(2)],
        ],
        compiler_params=pltpu.CompilerParams(
            collective_id=0, has_side_effects=True, vmem_limit_bytes=56 * 1024 * 1024
        ),
    )(features, weight, cotangent, tiles.reshape(rows, BLK), source, bid, key)


def solution(mesh):
    placed = (
        P(("rows", "rep"), None),
        P(),
        P("rows", "rep", None, None, None, None),
        P("rows", "rep", None, None),
        P("rows", "rep", None, None),
        P(("rows", "rep"), None),
    )
    return jax.shard_map(
        local,
        mesh=mesh,
        in_specs=placed,
        out_specs=(P(("rows", "rep"), None), P(), P(("rows", "rep"), None)),
        check_vma=False,
    )
```

```python
import math

import jax
import jax.numpy as jnp
from jax import lax
from jax.experimental import pallas as pl
from jax.experimental.pallas import tpu as pltpu
from jax.sharding import PartitionSpec as P

MESH = pl.DeviceIdType.MESH
BF = jnp.bfloat16
F32 = jnp.float32

NY, ZH, NC, ZL, NX = 8, 4, 2, 3, 4
NJ = NY * NC
NREP = ZL * NX
NM = NC * NX
NZ = ZH * ZL
SLOT = 24
MSG = ZH * SLOT
BLK = 128
F = 256
PER_COL = 8
NCOL = 12
NODES = 98304


def _copy(src, dst, ssem, rsem, rows, rep):
    return pltpu.make_async_remote_copy(
        src_ref=src,
        dst_ref=dst,
        send_sem=ssem,
        recv_sem=rsem,
        device_id=(rows, rep),
        device_id_type=MESH,
    )


def _kernel(
    feat, weight, cot, tiles, src, meta,
    out, gw, gx,
    X, tb, tf, G, A, AT, keys, U, T, s1, r1, acc, s2, r2, BI, s3, R, ts, town, rs,
    W, WA, w1, WB, WC, WD, WE,
    loc_sem, ag_s, ag_r, k_s, k_r, y1_s, y1_r, z1_s, z1_r, z2_s, z2_r, y2_s, y2_r,
    rs_s, rs_r, a_s, a_r, b_s, b_r, c_s, c_r, d_s, d_r, e_s, e_r,
):
    r = lax.axis_index("rows")
    c = lax.axis_index("rep")
    y, zh, core = lax.div(r, ZH * NC), lax.rem(lax.div(r, NC), ZH), lax.rem(r, NC)
    zl, x = lax.div(c, NX), lax.rem(c, NX)
    j = y * NC + core
    m = core * NX + x
    z = zh * ZL + zl

    def row_of(yy, hh, cc):
        return (yy * ZH + hh) * NC + cc

    def plane(jj):
        return row_of(lax.div(jj, NC), zh, lax.rem(jj, NC)), c

    def column(hh):
        return row_of(y, hh, core), c

    def pair(mm):
        return row_of(y, zh, lax.div(mm, NX)), zl * NX + lax.rem(mm, NX)

    def along_y(yy):
        return row_of(yy, zh, core), c

    def along_z(zz):
        return row_of(y, lax.div(zz, ZL), core), lax.rem(zz, ZL) * NX + x

    def each(count, me, fn):
        def step(k, carry):
            fn(lax.rem(me + k, count))
            return carry

        lax.fori_loop(1, count, step, 0)

    def ag(h):
        return lambda o, own: _copy(X.at[h, c], X.at[h, own], ag_s.at[h, o], ag_r.at[h, own], r, o)

    def y1(h):
        return lambda o, own: _copy(
            s1.at[h, o], r1.at[h, own, pl.ds(0, MSG)], y1_s.at[h, o], y1_r.at[h, own], *plane(o)
        )

    def z1(h):
        return lambda o, own: _copy(
            s2.at[h, o], r2.at[h, own], z1_s.at[h, o], z1_r.at[h, own], *column(o)
        )

    def z2(h):
        return lambda o, own: _copy(
            BI.at[h, zh], BI.at[h, own], z2_s.at[h, o], z2_r.at[h, own], *column(o)
        )

    def y2(h):
        return lambda o, own: _copy(
            s3.at[h, o], R.at[h, own, pl.ds(0, MSG)], y2_s.at[h, o], y2_r.at[h, own], *plane(o)
        )

    def rx(h):
        return lambda o, own: _copy(
            ts.at[h, o], rs.at[h, own], rs_s.at[h, o], rs_r.at[h, own], r, o
        )

    def kx(o, own):
        return _copy(meta.at[NJ + o], keys.at[own], k_s.at[o], k_r.at[own], *plane(o))

    def ga(o, own):
        return _copy(W.at[o], WA.at[own], a_s.at[o], a_r.at[own], *pair(o))

    def gb(o, own):
        return _copy(w1.at[o], WB.at[own], b_s.at[o], b_r.at[own], *along_y(o))

    def gc(o, own):
        return _copy(WC.at[z], WC.at[own], c_s.at[o], c_r.at[own], *along_z(o))

    def gd(o, own):
        return _copy(WD.at[y], WD.at[own], d_s.at[o], d_r.at[own], *along_y(o))

    def ge(o, own):
        return _copy(WE.at[m], WE.at[own], e_s.at[o], e_r.at[own], *pair(o))

    def start(make, count, me):
        each(count, me, lambda o: make(o, me).start())

    def arrive(make, count, me):
        each(count, me, lambda o: make(o, o).wait_recv())

    def sent(make, count, me):
        each(count, me, lambda o: make(o, me).wait_send())

    load = pltpu.make_async_copy(tiles, tb, loc_sem)
    load.start()

    barrier = pltpu.get_barrier_semaphore()

    def greet(rows, rep):
        pl.semaphore_signal(barrier, inc=1, device_id=(rows, rep), device_id_type=MESH)

    each(NREP, c, lambda cc: greet(r, cc))
    each(NJ, j, lambda jj: greet(*plane(jj)))
    each(ZH, zh, lambda hh: greet(*column(hh)))
    each(NX, x, lambda xx: greet(row_of(y, zh, 1 - core), zl * NX + xx))
    each(ZH, zh, lambda hh: each(ZL, zl, lambda ll: greet(row_of(y, hh, core), ll * NX + x)))
    for h in range(2):
        X[h, c] = feat[:, h * BLK : (h + 1) * BLK]
    pl.semaphore_wait(barrier, (NREP - 1) + (NJ - 1) + (ZH - 1) + (NX - 1) + (ZH - 1) * (ZL - 1))

    for h in range(2):
        start(ag(h), NREP, c)
    start(kx, NJ, j)
    keys[j] = meta[NJ + j]

    def clear(jj, carry):
        for h in range(2):
            r1[h, jj, MSG:BLK, :] = jnp.zeros((BLK - MSG, BLK), BF)
            R[h, jj, MSG:BLK, :] = jnp.zeros((BLK - MSG, BLK), BF)
        return carry

    lax.fori_loop(0, NJ, clear, 0)

    load.wait()

    def widen(t, carry):
        at = pl.multiple_of(t * BLK, BLK)
        tf[pl.ds(at, BLK), :] = tb[pl.ds(at, BLK), :].astype(F32)
        return carry

    lax.fori_loop(0, NCOL * PER_COL, widen, 0)

    def block_of(jj):
        return lax.shift_right_arithmetic(meta[jj], 10).astype(F32)

    def column_of(row):
        return jnp.transpose(jnp.broadcast_to(row, (BLK, BLK)))

    def gather(jj, carry):
        for i in range(MSG):
            G[jj, i : i + 1, :] = tf[pl.ds(src[jj, i], 1), :]
        rows = G[jj, 0:MSG, :]
        where = column_of(block_of(jj))[0:MSG, :]
        for b in range(NCOL):
            A[jj, :, b * BLK : (b + 1) * BLK] = jnp.where(where == b, rows, 0.0).astype(BF)
        return carry

    lax.fori_loop(0, NJ, gather, 0)

    def fan_out(h, left, right, width, held, make):
        for t in range(NJ // 4):
            at = lax.rem(lax.div(j, 4) + t, 4) * 4
            rows = jnp.dot(
                left[pl.ds(at, 4)].reshape(4 * MSG, width), right, preferred_element_type=F32
            )
            held[h, pl.ds(at, 4)] = rows.reshape(4, MSG, BLK).astype(BF)
            for u in range(4):
                o = at + lax.rem(j + u, 4)

                @pl.when(o != j)
                def _():
                    make(o, j).start()

    for h in range(2):
        arrive(ag(h), NREP, c)
        fan_out(h, A, X[h].reshape(NREP * BLK, BLK), NREP * BLK, s1, y1(h))
        r1[h, j, 0:MSG, :] = s1[h, j]

    arrive(kx, NJ, j)
    lanes = lax.broadcasted_iota(jnp.int32, (MSG, BLK), 1).astype(F32)
    heads = lax.broadcasted_iota(jnp.int32, (ZH * BLK, BLK), 0)

    def mirror(jj, carry):
        at = pl.multiple_of(jj * BLK, BLK)
        T[:, pl.ds(at, BLK)] = jnp.where(keys[jj] == heads, 1.0, 0.0).astype(BF)
        where = column_of(keys[jj].astype(F32))[0:MSG, :]
        for h in range(ZH):
            U[jj, :, h * BLK : (h + 1) * BLK] = jnp.where(
                where == lanes + float(h * BLK), 1.0, 0.0
            ).astype(BF)
        turned = jnp.transpose(G[jj])
        row = block_of(jj)
        for b in range(NCOL):
            AT[b, :, pl.ds(at, BLK)] = jnp.where(row == b, turned, 0.0).astype(BF)
        return carry

    lax.fori_loop(0, NJ, mirror, 0)

    for h in range(2):
        arrive(y1(h), NJ, j)
        acc[h] = jnp.dot(
            T[...], r1[h].reshape(NJ * BLK, BLK), preferred_element_type=F32
        ).reshape(ZH, BLK, BLK)
        for k in range(1, ZH):
            o = lax.rem(zh + k, ZH)
            s2[h, o] = acc[h, o].astype(BF)
            z1(h)(o, zh).start()

    halves = []
    for h in range(2):
        total = feat[:, h * BLK : (h + 1) * BLK].astype(F32) + acc[h, zh]
        arrive(z1(h), ZH, zh)
        for k in range(1, ZH):
            total += r2[h, lax.rem(zh + k, ZH)].astype(F32)
        halves.append(total.astype(BF))
    aggregated = jnp.concatenate(halves, axis=1)

    preact = jnp.dot(aggregated, weight[...], preferred_element_type=F32)
    sigmoid = jax.nn.sigmoid(preact)
    pre_grad = (cot[...].astype(F32) * sigmoid * (1.0 + preact * (1.0 - sigmoid))).astype(BF)
    back_in = lax.dot_general(
        pre_grad, weight[...], (((1,), (1,)), ((), ())), preferred_element_type=F32
    ).astype(BF)
    for h in range(2):
        BI[h, zh] = back_in[:, h * BLK : (h + 1) * BLK]
        start(z2(h), ZH, zh)

    local_w = lax.dot_general(
        aggregated, pre_grad, (((0,), (0,)), ((), ())), preferred_element_type=F32
    )
    W[0 : NM // 2] = local_w[:, 0:BLK].reshape(NM // 2, NY, 8, BLK)
    W[NM // 2 : NM] = local_w[:, BLK:F].reshape(NM // 2, NY, 8, BLK)
    start(ga, NM, m)
    out[...] = (preact * sigmoid).astype(BF)
    arrive(ga, NM, m)
    total = W[m]
    for k in range(1, NM):
        total += WA[lax.rem(m + k, NM)]
    w1[...] = total
    start(gb, NY, y)

    for h in range(2):
        arrive(z2(h), ZH, zh)
        fan_out(h, U, BI[h].reshape(ZH * BLK, BLK), ZH * BLK, s3, y2(h))
        R[h, j, 0:MSG, :] = s3[h, j]

    arrive(gb, NY, y)
    total = w1[y]
    for k in range(1, NY):
        total += WB[lax.rem(y + k, NY)]
    WC[z] = total
    start(gc, NZ, z)
    arrive(gc, NZ, z)
    total = WC[0]
    for k in range(1, NZ):
        total += WC[k]
    WD[y] = total * (1.0 / math.sqrt(NODES))
    start(gd, NY, y)

    for h in range(2):
        arrive(y2(h), NJ, j)
        for t in range(ZL):
            at = lax.rem(zl + t, ZL) * NX
            terms = jnp.dot(
                AT[pl.ds(at, NX)].reshape(NX * BLK, NJ * BLK),
                R[h].reshape(NJ * BLK, BLK),
                preferred_element_type=F32,
            ).reshape(NX, BLK, BLK)
            ts[h, pl.ds(at, NX)] = terms.astype(BF)
            if t == 0:
                town[h] = terms
            for u in range(NX):
                o = at + lax.rem(x + u, NX)

                @pl.when(o != c)
                def _():
                    rx(h)(o, c).start()

        if h == 0:
            arrive(gd, NY, y)
            WE[m] = WD[...]
            start(ge, NM, m)

    for h in range(2):
        result = BI[h, zh].astype(F32) + town[h, x]
        arrive(rx(h), NREP, c)
        for k in range(1, NREP):
            result += rs[h, lax.rem(c + k, NREP)].astype(F32)
        gx[:, h * BLK : (h + 1) * BLK] = result.astype(BF)

    arrive(ge, NM, m)
    for h in range(2):
        gw[:, h * BLK : (h + 1) * BLK] = WE[h * NM // 2 : (h + 1) * NM // 2].reshape(F, BLK)

    for make, count, me in (
        (ag, NREP, c), (y1, NJ, j), (z1, ZH, zh), (z2, ZH, zh), (y2, NJ, j), (rx, NREP, c),
    ):
        for h in range(2):
            sent(make(h), count, me)
    for make, count, me in (
        (kx, NJ, j), (ga, NM, m), (gb, NY, y), (gc, NZ, z), (gd, NY, y), (ge, NM, m),
    ):
        sent(make, count, me)


def _leave(a, b, c, aa, bb, cc, sems):
    copies = [
        pltpu.make_async_copy(s, d, sems.at[i]) for i, (s, d) in enumerate(((a, aa), (b, bb), (c, cc)))
    ]
    for copy in copies:
        copy.start()
    for copy in copies:
        copy.wait()


def local(features, weight, tiles, send_src, send_dst, cotangent):
    head = jnp.arange(ZH, dtype=jnp.int32)[None, :, None, None] * BLK
    target = send_dst[0, 0].reshape(NY, ZH, NC, SLOT)
    key = jnp.where(target < BLK, target + head, -1)
    both = jnp.stack([send_src[0, 0].reshape(NY, ZH, NC, SLOT), key])
    both = both.transpose(0, 1, 3, 2, 4).reshape(2 * NJ, MSG)
    both = jnp.pad(both, ((0, 0), (0, BLK - MSG)), constant_values=-1)
    V = pltpu.VMEM
    dma = pltpu.SemaphoreType.DMA
    vmem = pl.BlockSpec(memory_space=pltpu.VMEM)
    hbm = pl.BlockSpec(memory_space=pl.ANY)
    rows = NCOL * PER_COL * BLK
    shapes = (
        jax.ShapeDtypeStruct((BLK, F), BF),
        jax.ShapeDtypeStruct((F, F), F32),
        jax.ShapeDtypeStruct((BLK, F), BF),
    )
    outs = pl.pallas_call(
        _kernel,
        out_shape=shapes,
        in_specs=[vmem, vmem, vmem, hbm, pl.BlockSpec(memory_space=pltpu.SMEM), vmem],
        out_specs=(vmem, vmem, vmem),
        scratch_shapes=[
            V((2, NREP, BLK, BLK), BF),
            V((rows, BLK), BF),
            V((rows, BLK), F32),
            V((NJ, BLK, BLK), F32),
            V((NJ, MSG, NCOL * BLK), BF),
            V((NCOL, BLK, NJ * BLK), BF),
            V((NJ, 1, BLK), jnp.int32),
            V((NJ, MSG, ZH * BLK), BF),
            V((ZH * BLK, NJ * BLK), BF),
            V((2, NJ, MSG, BLK), BF),
            V((2, NJ, BLK, BLK), BF),
            V((2, ZH, BLK, BLK), F32),
            V((2, ZH, BLK, BLK), BF),
            V((2, ZH, BLK, BLK), BF),
            V((2, ZH, BLK, BLK), BF),
            V((2, NJ, MSG, BLK), BF),
            V((2, NJ, BLK, BLK), BF),
            V((2, NREP, BLK, BLK), BF),
            V((2, NX, BLK, BLK), F32),
            V((2, NREP, BLK, BLK), BF),
            V((NM, NY, 8, BLK), F32),
            V((NM, NY, 8, BLK), F32),
            V((NY, 8, BLK), F32),
            V((NY, 8, BLK), F32),
            V((NZ, 8, BLK), F32),
            V((NY, 8, BLK), F32),
            V((NM, NY, 8, BLK), F32),
            dma,
            dma((2, NREP)), dma((2, NREP)), dma((NJ,)), dma((NJ,)), dma((2, NJ)), dma((2, NJ)),
            dma((2, ZH)), dma((2, ZH)), dma((2, ZH)), dma((2, ZH)), dma((2, NJ)), dma((2, NJ)),
            dma((2, NREP)), dma((2, NREP)),
            *[dma((n,)) for n in (NM, NY, NZ, NY, NM) for _ in range(2)],
        ],
        compiler_params=pltpu.CompilerParams(
            collective_id=0, has_side_effects=True, vmem_limit_bytes=56 * 1024 * 1024
        ),
    )(features, weight, cotangent, tiles.reshape(rows, BLK), both, both.reshape(2 * NJ, 1, BLK))
    return pl.pallas_call(
        _leave,
        out_shape=shapes,
        in_specs=[hbm] * 3,
        out_specs=(hbm,) * 3,
        scratch_shapes=[dma((3,))],
    )(*outs)


def solution(mesh):
    placed = (
        P(("rows", "rep"), None),
        P(),
        P("rows", "rep", None, None, None, None),
        P("rows", "rep", None, None),
        P("rows", "rep", None, None),
        P(("rows", "rep"), None),
    )
    return jax.shard_map(
        local,
        mesh=mesh,
        in_specs=placed,
        out_specs=(P(("rows", "rep"), None), P(), P(("rows", "rep"), None)),
        check_vma=False,
    )
```

```python
import math

import jax
import jax.numpy as jnp
from jax import lax
from jax.experimental import pallas as pl
from jax.experimental.pallas import tpu as pltpu
from jax.sharding import PartitionSpec as P

MESH = pl.DeviceIdType.MESH
BF = jnp.bfloat16
F32 = jnp.float32

NY, ZH, NC, ZL, NX = 8, 4, 2, 3, 4
NJ = NY * NC
NREP = ZL * NX
NM = NC * NX
NZ = ZH * ZL
SLOT = 24
MSG = ZH * SLOT
BLK = 128
F = 256
PER_COL = 8
NCOL = 12
NODES = 98304


def _copy(src, dst, ssem, rsem, rows, rep):
    return pltpu.make_async_remote_copy(
        src_ref=src,
        dst_ref=dst,
        send_sem=ssem,
        recv_sem=rsem,
        device_id=(rows, rep),
        device_id_type=MESH,
    )


def _kernel(
    feat, weight, cot, tiles, src, srcs, dsts,
    out, gw, gx,
    X, tb, tf, G, A, AT, bcol, brow, krow, keys, U, T, s1, r1, acc, s2, r2, BI, s3, R, ts, town, rs,
    W, WA, w1, WB, WC, WD, WE,
    loc_sem, ag_s, ag_r, k_s, k_r, y1_s, y1_r, z1_s, z1_r, z2_s, z2_r, y2_s, y2_r,
    rs_s, rs_r, a_s, a_r, b_s, b_r, c_s, c_r, d_s, d_r, e_s, e_r,
):
    r = lax.axis_index("rows")
    c = lax.axis_index("rep")
    y, zh, core = lax.div(r, ZH * NC), lax.rem(lax.div(r, NC), ZH), lax.rem(r, NC)
    zl, x = lax.div(c, NX), lax.rem(c, NX)
    j = y * NC + core
    m = core * NX + x
    z = zh * ZL + zl

    def row_of(yy, hh, cc):
        return (yy * ZH + hh) * NC + cc

    def plane(jj):
        return row_of(lax.div(jj, NC), zh, lax.rem(jj, NC)), c

    def column(hh):
        return row_of(y, hh, core), c

    def pair(mm):
        return row_of(y, zh, lax.div(mm, NX)), zl * NX + lax.rem(mm, NX)

    def along_y(yy):
        return row_of(yy, zh, core), c

    def along_z(zz):
        return row_of(y, lax.div(zz, ZL), core), lax.rem(zz, ZL) * NX + x

    def each(count, me, fn):
        def step(k, carry):
            fn(lax.rem(me + k, count))
            return carry

        lax.fori_loop(1, count, step, 0)

    def ag(h):
        return lambda o, own: _copy(X.at[h, c], X.at[h, own], ag_s.at[h, o], ag_r.at[h, own], r, o)

    def y1(h):
        return lambda o, own: _copy(
            s1.at[h, o], r1.at[h, own, pl.ds(0, MSG)], y1_s.at[h, o], y1_r.at[h, own], *plane(o)
        )

    def z1(h):
        return lambda o, own: _copy(
            s2.at[h, o], r2.at[h, own], z1_s.at[h, o], z1_r.at[h, own], *column(o)
        )

    def z2(h):
        return lambda o, own: _copy(
            BI.at[h, zh], BI.at[h, own], z2_s.at[h, o], z2_r.at[h, own], *column(o)
        )

    def y2(h):
        return lambda o, own: _copy(
            s3.at[h, o], R.at[h, own, pl.ds(0, MSG)], y2_s.at[h, o], y2_r.at[h, own], *plane(o)
        )

    def rx(h):
        return lambda o, own: _copy(
            ts.at[h, o], rs.at[h, own], rs_s.at[h, o], rs_r.at[h, own], r, o
        )

    def kx(o, own):
        return _copy(krow.at[o], keys.at[own], k_s.at[o], k_r.at[own], *plane(o))

    def ga(o, own):
        return _copy(W.at[o], WA.at[own], a_s.at[o], a_r.at[own], *pair(o))

    def gb(o, own):
        return _copy(w1.at[o], WB.at[own], b_s.at[o], b_r.at[own], *along_y(o))

    def gc(o, own):
        return _copy(WC.at[z], WC.at[own], c_s.at[o], c_r.at[own], *along_z(o))

    def gd(o, own):
        return _copy(WD.at[y], WD.at[own], d_s.at[o], d_r.at[own], *along_y(o))

    def ge(o, own):
        return _copy(WE.at[m], WE.at[own], e_s.at[o], e_r.at[own], *pair(o))

    def start(make, count, me):
        each(count, me, lambda o: make(o, me).start())

    def arrive(make, count, me):
        each(count, me, lambda o: make(o, o).wait_recv())

    def sent(make, count, me):
        each(count, me, lambda o: make(o, me).wait_send())

    load = pltpu.make_async_copy(tiles, tb, loc_sem)
    load.start()

    barrier = pltpu.get_barrier_semaphore()

    def greet(rows, rep):
        pl.semaphore_signal(barrier, inc=1, device_id=(rows, rep), device_id_type=MESH)

    each(NREP, c, lambda cc: greet(r, cc))
    each(NJ, j, lambda jj: greet(*plane(jj)))
    each(ZH, zh, lambda hh: greet(*column(hh)))
    each(NX, x, lambda xx: greet(row_of(y, zh, 1 - core), zl * NX + xx))
    each(ZH, zh, lambda hh: each(ZL, zl, lambda ll: greet(row_of(y, hh, core), ll * NX + x)))
    for h in range(2):
        X[h, c] = feat[:, h * BLK : (h + 1) * BLK]
    pl.semaphore_wait(barrier, (NREP - 1) + (NJ - 1) + (ZH - 1) + (NX - 1) + (ZH - 1) * (ZL - 1))

    for h in range(2):
        start(ag(h), NREP, c)

    def clear(jj, carry):
        for h in range(2):
            r1[h, jj, MSG:BLK, :] = jnp.zeros((BLK - MSG, BLK), BF)
            R[h, jj, MSG:BLK, :] = jnp.zeros((BLK - MSG, BLK), BF)
        return carry

    lax.fori_loop(0, NJ, clear, 0)

    load.wait()

    def widen(t, carry):
        at = pl.multiple_of(t * BLK, BLK)
        tf[pl.ds(at, BLK), :] = tb[pl.ds(at, BLK), :].astype(F32)
        return carry

    lax.fori_loop(0, NCOL * PER_COL, widen, 0)

    block = lax.shift_right_arithmetic(srcs[...], 10).astype(F32)
    landing = dsts[...].astype(F32)
    padding = jnp.full((BLK - MSG, BLK), -1.0, F32)
    for jj in range(NJ):
        peers = [((jj // NC) * ZH + h) * NC + jj % NC for h in range(ZH)]
        blocks = [jnp.broadcast_to(block[:, p : p + 1], (SLOT, BLK)) for p in peers]
        heads = [jnp.broadcast_to(landing[:, p : p + 1], (SLOT, BLK)) for p in peers]
        heads = [jnp.where(v < BLK, v + float(h * BLK), -1.0) for h, v in enumerate(heads)]
        blocks = jnp.concatenate([*blocks, padding], axis=0)
        bcol[jj] = blocks[0:MSG]
        brow[jj] = jnp.transpose(blocks)[0:1]
        krow[jj] = jnp.transpose(jnp.concatenate([*heads, padding], axis=0))[0:1]
    start(kx, NJ, j)
    keys[j] = krow[j]

    def gather(jj, carry):
        first = lax.div(jj, NC) * (ZH * NC) + lax.rem(jj, NC)
        for h in range(ZH):
            for i in range(SLOT):
                at = h * SLOT + i
                G[jj, at : at + 1, :] = tf[pl.ds(src[i, first + h * NC], 1), :]
        rows = G[jj, 0:MSG, :]
        where = bcol[jj]
        for b in range(NCOL):
            A[jj, :, b * BLK : (b + 1) * BLK] = jnp.where(where == b, rows, 0.0).astype(BF)
        return carry

    lax.fori_loop(0, NJ, gather, 0)

    def fan_out(h, left, right, width, held, make):
        for t in range(NJ // 4):
            at = lax.rem(lax.div(j, 4) + t, 4) * 4
            rows = jnp.dot(
                left[pl.ds(at, 4)].reshape(4 * MSG, width), right, preferred_element_type=F32
            )
            held[h, pl.ds(at, 4)] = rows.reshape(4, MSG, BLK).astype(BF)
            for u in range(4):
                o = at + lax.rem(j + u, 4)

                @pl.when(o != j)
                def _():
                    make(o, j).start()

    for h in range(2):
        arrive(ag(h), NREP, c)
        fan_out(h, A, X[h].reshape(NREP * BLK, BLK), NREP * BLK, s1, y1(h))
        r1[h, j, 0:MSG, :] = s1[h, j]

    arrive(kx, NJ, j)
    lanes = lax.broadcasted_iota(jnp.int32, (MSG, BLK), 1).astype(F32)
    heads = lax.broadcasted_iota(jnp.int32, (ZH * BLK, BLK), 0).astype(F32)

    def mirror(jj, carry):
        at = pl.multiple_of(jj * BLK, BLK)
        T[:, pl.ds(at, BLK)] = jnp.where(keys[jj] == heads, 1.0, 0.0).astype(BF)
        where = jnp.transpose(jnp.broadcast_to(keys[jj], (BLK, BLK)))[0:MSG, :]
        for h in range(ZH):
            U[jj, :, h * BLK : (h + 1) * BLK] = jnp.where(
                where == lanes + float(h * BLK), 1.0, 0.0
            ).astype(BF)
        turned = jnp.transpose(G[jj])
        row = brow[jj]
        for b in range(NCOL):
            AT[b, :, pl.ds(at, BLK)] = jnp.where(row == b, turned, 0.0).astype(BF)
        return carry

    lax.fori_loop(0, NJ, mirror, 0)

    for h in range(2):
        arrive(y1(h), NJ, j)
        acc[h] = jnp.dot(
            T[...], r1[h].reshape(NJ * BLK, BLK), preferred_element_type=F32
        ).reshape(ZH, BLK, BLK)
        for k in range(1, ZH):
            o = lax.rem(zh + k, ZH)
            s2[h, o] = acc[h, o].astype(BF)
            z1(h)(o, zh).start()

    halves = []
    for h in range(2):
        total = feat[:, h * BLK : (h + 1) * BLK].astype(F32) + acc[h, zh]
        arrive(z1(h), ZH, zh)
        for k in range(1, ZH):
            total += r2[h, lax.rem(zh + k, ZH)].astype(F32)
        halves.append(total.astype(BF))
    aggregated = jnp.concatenate(halves, axis=1)

    preact = jnp.dot(aggregated, weight[...], preferred_element_type=F32)
    sigmoid = jax.nn.sigmoid(preact)
    pre_grad = (cot[...].astype(F32) * sigmoid * (1.0 + preact * (1.0 - sigmoid))).astype(BF)
    back_in = lax.dot_general(
        pre_grad, weight[...], (((1,), (1,)), ((), ())), preferred_element_type=F32
    ).astype(BF)
    for h in range(2):
        BI[h, zh] = back_in[:, h * BLK : (h + 1) * BLK]
        start(z2(h), ZH, zh)

    local_w = lax.dot_general(
        aggregated, pre_grad, (((0,), (0,)), ((), ())), preferred_element_type=F32
    )
    W[0 : NM // 2] = local_w[:, 0:BLK].reshape(NM // 2, NY, 8, BLK)
    W[NM // 2 : NM] = local_w[:, BLK:F].reshape(NM // 2, NY, 8, BLK)
    start(ga, NM, m)
    out[...] = (preact * sigmoid).astype(BF)
    arrive(ga, NM, m)
    total = W[m]
    for k in range(1, NM):
        total += WA[lax.rem(m + k, NM)]
    w1[...] = total
    start(gb, NY, y)

    for h in range(2):
        arrive(z2(h), ZH, zh)
        fan_out(h, U, BI[h].reshape(ZH * BLK, BLK), ZH * BLK, s3, y2(h))
        R[h, j, 0:MSG, :] = s3[h, j]

    arrive(gb, NY, y)
    total = w1[y]
    for k in range(1, NY):
        total += WB[lax.rem(y + k, NY)]
    WC[z] = total
    start(gc, NZ, z)
    arrive(gc, NZ, z)
    total = WC[0]
    for k in range(1, NZ):
        total += WC[k]
    WD[y] = total * (1.0 / math.sqrt(NODES))
    start(gd, NY, y)

    for h in range(2):
        arrive(y2(h), NJ, j)
        for t in range(ZL):
            at = lax.rem(zl + t, ZL) * NX
            terms = jnp.dot(
                AT[pl.ds(at, NX)].reshape(NX * BLK, NJ * BLK),
                R[h].reshape(NJ * BLK, BLK),
                preferred_element_type=F32,
            ).reshape(NX, BLK, BLK)
            ts[h, pl.ds(at, NX)] = terms.astype(BF)
            if t == 0:
                town[h] = terms
            for u in range(NX):
                o = at + lax.rem(x + u, NX)

                @pl.when(o != c)
                def _():
                    rx(h)(o, c).start()

        if h == 0:
            arrive(gd, NY, y)
            WE[m] = WD[...]
            start(ge, NM, m)

    for h in range(2):
        result = BI[h, zh].astype(F32) + town[h, x]
        arrive(rx(h), NREP, c)
        for k in range(1, NREP):
            result += rs[h, lax.rem(c + k, NREP)].astype(F32)
        gx[:, h * BLK : (h + 1) * BLK] = result.astype(BF)

    arrive(ge, NM, m)
    for h in range(2):
        gw[:, h * BLK : (h + 1) * BLK] = WE[h * NM // 2 : (h + 1) * NM // 2].reshape(F, BLK)

    for make, count, me in (
        (ag, NREP, c), (y1, NJ, j), (z1, ZH, zh), (z2, ZH, zh), (y2, NJ, j), (rx, NREP, c),
    ):
        for h in range(2):
            sent(make(h), count, me)
    for make, count, me in (
        (kx, NJ, j), (ga, NM, m), (gb, NY, y), (gc, NZ, z), (gd, NY, y), (ge, NM, m),
    ):
        sent(make, count, me)


def _leave(a, b, c, aa, bb, cc):
    aa[...] = a[...]
    bb[...] = b[...]
    cc[...] = c[...]


def local(features, weight, tiles, send_src, send_dst, cotangent):
    source = send_src[0, 0].T
    target = send_dst[0, 0].T
    V = pltpu.VMEM
    dma = pltpu.SemaphoreType.DMA
    vmem = pl.BlockSpec(memory_space=pltpu.VMEM)
    hbm = pl.BlockSpec(memory_space=pl.ANY)
    rows = NCOL * PER_COL * BLK
    shapes = (
        jax.ShapeDtypeStruct((BLK, F), BF),
        jax.ShapeDtypeStruct((F, F), F32),
        jax.ShapeDtypeStruct((BLK, F), BF),
    )
    outs = pl.pallas_call(
        _kernel,
        out_shape=shapes,
        in_specs=[vmem, vmem, vmem, hbm, pl.BlockSpec(memory_space=pltpu.SMEM), vmem, vmem],
        out_specs=(vmem, vmem, vmem),
        scratch_shapes=[
            V((2, NREP, BLK, BLK), BF),
            V((rows, BLK), BF),
            V((rows, BLK), F32),
            V((NJ, BLK, BLK), F32),
            V((NJ, MSG, NCOL * BLK), BF),
            V((NCOL, BLK, NJ * BLK), BF),
            V((NJ, MSG, BLK), F32),
            V((NJ, 1, BLK), F32),
            V((NJ, 1, BLK), F32),
            V((NJ, 1, BLK), F32),
            V((NJ, MSG, ZH * BLK), BF),
            V((ZH * BLK, NJ * BLK), BF),
            V((2, NJ, MSG, BLK), BF),
            V((2, NJ, BLK, BLK), BF),
            V((2, ZH, BLK, BLK), F32),
            V((2, ZH, BLK, BLK), BF),
            V((2, ZH, BLK, BLK), BF),
            V((2, ZH, BLK, BLK), BF),
            V((2, NJ, MSG, BLK), BF),
            V((2, NJ, BLK, BLK), BF),
            V((2, NREP, BLK, BLK), BF),
            V((2, NX, BLK, BLK), F32),
            V((2, NREP, BLK, BLK), BF),
            V((NM, NY, 8, BLK), F32),
            V((NM, NY, 8, BLK), F32),
            V((NY, 8, BLK), F32),
            V((NY, 8, BLK), F32),
            V((NZ, 8, BLK), F32),
            V((NY, 8, BLK), F32),
            V((NM, NY, 8, BLK), F32),
            dma,
            dma((2, NREP)), dma((2, NREP)), dma((NJ,)), dma((NJ,)), dma((2, NJ)), dma((2, NJ)),
            dma((2, ZH)), dma((2, ZH)), dma((2, ZH)), dma((2, ZH)), dma((2, NJ)), dma((2, NJ)),
            dma((2, NREP)), dma((2, NREP)),
            *[dma((n,)) for n in (NM, NY, NZ, NY, NM) for _ in range(2)],
        ],
        compiler_params=pltpu.CompilerParams(
            collective_id=0, has_side_effects=True, vmem_limit_bytes=56 * 1024 * 1024
        ),
    )(features, weight, cotangent, tiles.reshape(rows, BLK), source, source, target)
    return pl.pallas_call(
        _leave,
        out_shape=shapes,
        in_specs=[vmem] * 3,
        out_specs=(vmem,) * 3,
    )(*outs)


def solution(mesh):
    placed = (
        P(("rows", "rep"), None),
        P(),
        P("rows", "rep", None, None, None, None),
        P("rows", "rep", None, None),
        P("rows", "rep", None, None),
        P(("rows", "rep"), None),
    )
    return jax.shard_map(
        local,
        mesh=mesh,
        in_specs=placed,
        out_specs=(P(("rows", "rep"), None), P(), P(("rows", "rep"), None)),
        check_vma=False,
    )
```

```python
import math

import jax
import jax.numpy as jnp
from jax import lax
from jax.experimental import pallas as pl
from jax.experimental.pallas import tpu as pltpu
from jax.sharding import PartitionSpec as P

MESH = pl.DeviceIdType.MESH
BF = jnp.bfloat16
F32 = jnp.float32

NY, ZH, NC, ZL, NX = 8, 4, 2, 3, 4
NJ = NY * NC
NREP = ZL * NX
NM = NC * NX
NZ = ZH * ZL
SLOT = 24
MSG = ZH * SLOT
OTHER = MSG - SLOT
OWN = ZH - 1
BLK = 128
F = 256
PER_COL = 8
NCOL = 12
NODES = 98304


def _copy(src, dst, ssem, rsem, rows, rep):
    return pltpu.make_async_remote_copy(
        src_ref=src,
        dst_ref=dst,
        send_sem=ssem,
        recv_sem=rsem,
        device_id=(rows, rep),
        device_id_type=MESH,
    )


def _kernel(
    feat, weight, cot, tiles, src, srcs, dsts,
    out, gw, gx,
    X, tb, tf, G, A, AT, bcol, brow, krow, nat, keys, U, Uo, T, s1, r1, ro, acc, s2, r2, BI, s3, so, R, ts, town, rs,
    W, WA, w1, WB, WC, WD, WE,
    loc_sem, ag_s, ag_r, k_s, k_r, y1_s, y1_r, o1_s, o1_r, z1_s, z1_r, z2_s, z2_r,
    y2_s, y2_r, o2_s, o2_r,
    rs_s, rs_r, a_s, a_r, b_s, b_r, c_s, c_r, d_s, d_r, e_s, e_r,
):
    r = lax.axis_index("rows")
    c = lax.axis_index("rep")
    y, zh, core = lax.div(r, ZH * NC), lax.rem(lax.div(r, NC), ZH), lax.rem(r, NC)
    zl, x = lax.div(c, NX), lax.rem(c, NX)
    j = y * NC + core
    m = core * NX + x
    z = zh * ZL + zl

    def row_of(yy, hh, cc):
        return (yy * ZH + hh) * NC + cc

    def plane(jj):
        return row_of(lax.div(jj, NC), zh, lax.rem(jj, NC)), c

    def column(hh):
        return row_of(y, hh, core), c

    def pair(mm):
        return row_of(y, zh, lax.div(mm, NX)), zl * NX + lax.rem(mm, NX)

    def along_y(yy):
        return row_of(yy, zh, core), c

    def along_z(zz):
        return row_of(y, lax.div(zz, ZL), core), lax.rem(zz, ZL) * NX + x

    def each(count, me, fn):
        def step(k, carry):
            fn(lax.rem(me + k, count))
            return carry

        lax.fori_loop(1, count, step, 0)

    def ag(h):
        return lambda o, own: _copy(X.at[h, c], X.at[h, own], ag_s.at[h, o], ag_r.at[h, own], r, o)

    def y1(h):
        return lambda o, own: _copy(
            s1.at[h, o, pl.ds(0, OTHER)], r1.at[h, own, pl.ds(0, OTHER)],
            y1_s.at[h, o], y1_r.at[h, own], *plane(o),
        )

    def o1(o, own):
        return _copy(
            s1.at[:, o, pl.ds(OTHER, SLOT)], ro.at[:, own, pl.ds(OTHER, SLOT)],
            o1_s.at[o], o1_r.at[own], *plane(o),
        )

    def place(q):
        return lax.rem(zh + 1 + q, ZH)

    def z1(h, q, at):
        return _copy(s2.at[h, q], r2.at[h, at], z1_s.at[h, q], z1_r.at[h, at], *column(place(q)))

    def z2(h, q, at):
        return _copy(BI.at[h, OWN], BI.at[h, at], z2_s.at[h, q], z2_r.at[h, at], *column(place(q)))

    def y2(h):
        return lambda o, own: _copy(
            s3.at[h, o], R.at[h, own, pl.ds(0, OTHER)], y2_s.at[h, o], y2_r.at[h, own], *plane(o)
        )

    def o2(o, own):
        return _copy(
            so.at[:, o], R.at[:, own, pl.ds(OTHER, SLOT)], o2_s.at[o], o2_r.at[own], *plane(o)
        )

    def rx(h):
        return lambda o, own: _copy(
            ts.at[h, o], rs.at[h, own], rs_s.at[h, o], rs_r.at[h, own], r, o
        )

    def kx(o, own):
        return _copy(krow.at[o], keys.at[own], k_s.at[o], k_r.at[own], *plane(o))

    def ga(o, own):
        return _copy(W.at[o], WA.at[own], a_s.at[o], a_r.at[own], *pair(o))

    def gb(o, own):
        return _copy(w1.at[o], WB.at[own], b_s.at[o], b_r.at[own], *along_y(o))

    def gc(o, own):
        return _copy(WC.at[z], WC.at[own], c_s.at[o], c_r.at[own], *along_z(o))

    def gd(o, own):
        return _copy(WD.at[y], WD.at[own], d_s.at[o], d_r.at[own], *along_y(o))

    def ge(o, own):
        return _copy(WE.at[m], WE.at[own], e_s.at[o], e_r.at[own], *pair(o))

    def start(make, count, me):
        each(count, me, lambda o: make(o, me).start())

    def arrive(make, count, me):
        each(count, me, lambda o: make(o, o).wait_recv())

    def sent(make, count, me):
        each(count, me, lambda o: make(o, me).wait_send())

    load = pltpu.make_async_copy(tiles, tb, loc_sem)
    load.start()

    barrier = pltpu.get_barrier_semaphore()

    def greet(rows, rep):
        pl.semaphore_signal(barrier, inc=1, device_id=(rows, rep), device_id_type=MESH)

    each(NREP, c, lambda cc: greet(r, cc))
    each(NJ, j, lambda jj: greet(*plane(jj)))
    each(ZH, zh, lambda hh: greet(*column(hh)))
    each(NX, x, lambda xx: greet(row_of(y, zh, 1 - core), zl * NX + xx))
    each(ZH, zh, lambda hh: each(ZL, zl, lambda ll: greet(row_of(y, hh, core), ll * NX + x)))
    for h in range(2):
        X[h, c] = feat[:, h * BLK : (h + 1) * BLK]
    pl.semaphore_wait(barrier, (NREP - 1) + (NJ - 1) + (ZH - 1) + (NX - 1) + (ZH - 1) * (ZL - 1))

    for h in range(2):
        start(ag(h), NREP, c)

    def clear(jj, carry):
        for h in range(2):
            r1[h, jj, OTHER:BLK, :] = jnp.zeros((BLK - OTHER, BLK), BF)
            ro[h, jj, 0:OTHER, :] = jnp.zeros((OTHER, BLK), BF)
            ro[h, jj, MSG:BLK, :] = jnp.zeros((BLK - MSG, BLK), BF)
            R[h, jj, MSG:BLK, :] = jnp.zeros((BLK - MSG, BLK), BF)
        return carry

    lax.fori_loop(0, NJ, clear, 0)

    load.wait()

    def widen(t, carry):
        at = pl.multiple_of(t * BLK, BLK)
        tf[pl.ds(at, BLK), :] = tb[pl.ds(at, BLK), :].astype(F32)
        return carry

    lax.fori_loop(0, NCOL * PER_COL, widen, 0)

    block = lax.shift_right_arithmetic(srcs[...], 10).astype(F32)
    landing = dsts[...].astype(F32)
    padding = jnp.full((BLK - MSG, BLK), -1.0, F32)
    for jj in range(NJ):
        peers = [((jj // NC) * ZH + h) * NC + jj % NC for h in range(ZH)]
        for h, p in enumerate(peers):
            nat[0, h * SLOT : (h + 1) * SLOT] = jnp.broadcast_to(block[:, p : p + 1], (SLOT, BLK))
            nat[1, h * SLOT : (h + 1) * SLOT] = jnp.broadcast_to(landing[:, p : p + 1], (SLOT, BLK))
        at = [pl.ds(pl.multiple_of(place(q) * SLOT, 8), SLOT) for q in range(ZH)]
        heads = [nat[1, at[q]] for q in range(ZH)]
        heads = [jnp.where(v < BLK, v + float(q * BLK), -1.0) for q, v in enumerate(heads)]
        blocks = jnp.concatenate([*[nat[0, at[q]] for q in range(ZH)], padding], axis=0)
        bcol[jj] = blocks[0:MSG]
        brow[jj] = jnp.transpose(blocks)[0:1]
        krow[jj] = jnp.transpose(jnp.concatenate([*heads, padding], axis=0))[0:1]
    start(kx, NJ, j)
    keys[j] = krow[j]

    def gather(jj, carry):
        first = lax.div(jj, NC) * (ZH * NC) + lax.rem(jj, NC)
        for q in range(ZH):
            peer = first + place(q) * NC
            for i in range(SLOT):
                at = q * SLOT + i
                G[jj, at : at + 1, :] = tf[pl.ds(src[i, peer], 1), :]
        rows = G[jj, 0:MSG, :]
        where = bcol[jj]
        for b in range(NCOL):
            A[jj, :, b * BLK : (b + 1) * BLK] = jnp.where(where == b, rows, 0.0).astype(BF)
        return carry

    lax.fori_loop(0, NJ, gather, 0)

    def fan_out(left, right, width, hold, make):
        for t in range(NJ // 4):
            at = lax.rem(lax.div(j, 4) + t, 4) * 4
            rows = jnp.dot(
                left[pl.ds(at, 4)].reshape(4 * MSG, width), right, preferred_element_type=F32
            )
            hold(pl.ds(at, 4), rows.reshape(4, MSG, BLK))
            for u in range(4):
                o = at + lax.rem(j + u, 4)

                @pl.when(o != j)
                def _():
                    make(o, j).start()

    for h in range(2):
        arrive(ag(h), NREP, c)

        def hold(at, rows):
            s1[h, at] = rows.astype(BF)

        fan_out(A, X[h].reshape(NREP * BLK, BLK), NREP * BLK, hold, y1(h))
        r1[h, j, 0:OTHER, :] = s1[h, j, 0:OTHER, :]
        ro[h, j, OTHER:MSG, :] = s1[h, j, OTHER:MSG, :]
    start(o1, NJ, j)

    arrive(kx, NJ, j)
    lanes = lax.broadcasted_iota(jnp.int32, (MSG, BLK), 1).astype(F32)
    heads = lax.broadcasted_iota(jnp.int32, (ZH * BLK, BLK), 0).astype(F32)

    def mirror(jj, carry):
        at = pl.multiple_of(jj * BLK, BLK)
        T[:, pl.ds(at, BLK)] = jnp.where(keys[jj] == heads, 1.0, 0.0).astype(BF)
        where = jnp.transpose(jnp.broadcast_to(keys[jj], (BLK, BLK)))
        for h in range(ZH):
            U[jj, :, h * BLK : (h + 1) * BLK] = jnp.where(
                where[0:MSG] == lanes + float(h * BLK), 1.0, 0.0
            ).astype(BF)
        Uo[jj] = jnp.where(
            where[OTHER : OTHER + 32] == lanes[0:32] + float(OWN * BLK), 1.0, 0.0
        ).astype(BF)
        turned = jnp.transpose(G[jj])
        row = brow[jj]
        for b in range(NCOL):
            AT[b, :, pl.ds(at, BLK)] = jnp.where(row == b, turned, 0.0).astype(BF)
        return carry

    lax.fori_loop(0, NJ, mirror, 0)

    for h in range(2):
        sent(ag(h), NREP, c)
    sent(kx, NJ, j)

    for h in range(2):
        arrive(y1(h), NJ, j)
        sums = jnp.dot(
            T[0 : OWN * BLK], r1[h].reshape(NJ * BLK, BLK), preferred_element_type=F32
        )
        for q in range(OWN):
            s2[h, q] = sums[q * BLK : (q + 1) * BLK].astype(BF)
            z1(h, q, OWN - 1 - q).start()

    arrive(o1, NJ, j)
    for h in range(2):
        acc[h] = feat[:, h * BLK : (h + 1) * BLK].astype(F32) + jnp.dot(
            T[OWN * BLK :], ro[h].reshape(NJ * BLK, BLK), preferred_element_type=F32
        )
    halves = []
    for h in range(2):
        total = acc[h]
        for q in range(OWN):
            z1(h, q, q).wait_recv()
        for q in range(OWN):
            total += r2[h, q].astype(F32)
        halves.append(total.astype(BF))
    aggregated = jnp.concatenate(halves, axis=1)

    preact = jnp.dot(aggregated, weight[...], preferred_element_type=F32)
    sigmoid = jax.nn.sigmoid(preact)
    pre_grad = (cot[...].astype(F32) * sigmoid * (1.0 + preact * (1.0 - sigmoid))).astype(BF)
    back_in = lax.dot_general(
        pre_grad, weight[...], (((1,), (1,)), ((), ())), preferred_element_type=F32
    ).astype(BF)
    for h in range(2):
        BI[h, OWN] = back_in[:, h * BLK : (h + 1) * BLK]
        for q in range(OWN):
            z2(h, q, OWN - 1 - q).start()
    for h in range(2):
        rows = jnp.dot(Uo[...].reshape(NJ * 32, BLK), BI[h, OWN], preferred_element_type=F32)
        so[h] = rows.reshape(NJ, 32, BLK)[:, 0:SLOT].astype(BF)
        R[h, j, OTHER:MSG, :] = so[h, j]
    start(o2, NJ, j)

    local_w = lax.dot_general(
        aggregated, pre_grad, (((0,), (0,)), ((), ())), preferred_element_type=F32
    )
    W[0 : NM // 2] = local_w[:, 0:BLK].reshape(NM // 2, NY, 8, BLK)
    W[NM // 2 : NM] = local_w[:, BLK:F].reshape(NM // 2, NY, 8, BLK)
    start(ga, NM, m)
    out[...] = (preact * sigmoid).astype(BF)
    arrive(ga, NM, m)
    total = W[m]
    for k in range(1, NM):
        total += WA[lax.rem(m + k, NM)]
    w1[...] = total
    start(gb, NY, y)

    for h in range(2):
        for q in range(OWN):
            z2(h, q, q).wait_recv()

        def hold(at, rows):
            s3[h, at] = rows[:, 0:OTHER].astype(BF)

        fan_out(U, BI[h].reshape(ZH * BLK, BLK), ZH * BLK, hold, y2(h))
        R[h, j, 0:OTHER, :] = s3[h, j]

    arrive(gb, NY, y)
    total = w1[y]
    for k in range(1, NY):
        total += WB[lax.rem(y + k, NY)]
    WC[z] = total
    start(gc, NZ, z)
    arrive(gc, NZ, z)
    total = WC[0]
    for k in range(1, NZ):
        total += WC[k]
    WD[y] = total * (1.0 / math.sqrt(NODES))
    start(gd, NY, y)

    for h in range(2):
        sent(y1(h), NJ, j)
        for q in range(OWN):
            z1(h, q, q).wait_send()
            z2(h, q, q).wait_send()
    sent(o1, NJ, j)
    sent(ga, NM, m)
    sent(gb, NY, y)
    sent(gc, NZ, z)

    arrive(o2, NJ, j)
    for h in range(2):
        arrive(y2(h), NJ, j)
        for t in range(ZL):
            at = lax.rem(zl + t, ZL) * NX
            terms = jnp.dot(
                AT[pl.ds(at, NX)].reshape(NX * BLK, NJ * BLK),
                R[h].reshape(NJ * BLK, BLK),
                preferred_element_type=F32,
            ).reshape(NX, BLK, BLK)
            ts[h, pl.ds(at, NX)] = terms.astype(BF)
            if t == 0:
                town[h] = terms
            for u in range(NX):
                o = at + lax.rem(x + u, NX)

                @pl.when(o != c)
                def _():
                    rx(h)(o, c).start()

        if h == 0:
            arrive(gd, NY, y)
            WE[m] = WD[...]
            start(ge, NM, m)
            sent(o2, NJ, j)
            sent(y2(0), NJ, j)

    sent(y2(1), NJ, j)
    sent(rx(0), NREP, c)
    sent(gd, NY, y)
    for h in range(2):
        result = BI[h, OWN].astype(F32) + town[h, x]
        arrive(rx(h), NREP, c)
        for k in range(1, NREP):
            result += rs[h, lax.rem(c + k, NREP)].astype(F32)
        gx[:, h * BLK : (h + 1) * BLK] = result.astype(BF)

    arrive(ge, NM, m)
    for h in range(2):
        gw[:, h * BLK : (h + 1) * BLK] = WE[h * NM // 2 : (h + 1) * NM // 2].reshape(F, BLK)

    sent(ge, NM, m)
    sent(rx(1), NREP, c)


def _leave(a, b, c, aa, bb, cc):
    aa[...] = a[...]
    bb[...] = b[...]
    cc[...] = c[...]


def local(features, weight, tiles, send_src, send_dst, cotangent):
    source = send_src[0, 0].T
    target = send_dst[0, 0].T
    V = pltpu.VMEM
    dma = pltpu.SemaphoreType.DMA
    vmem = pl.BlockSpec(memory_space=pltpu.VMEM)
    hbm = pl.BlockSpec(memory_space=pl.ANY)
    rows = NCOL * PER_COL * BLK
    shapes = (
        jax.ShapeDtypeStruct((BLK, F), BF),
        jax.ShapeDtypeStruct((F, F), F32),
        jax.ShapeDtypeStruct((BLK, F), BF),
    )
    outs = pl.pallas_call(
        _kernel,
        out_shape=shapes,
        in_specs=[vmem, vmem, vmem, hbm, pl.BlockSpec(memory_space=pltpu.SMEM), vmem, vmem],
        out_specs=(vmem, vmem, vmem),
        scratch_shapes=[
            V((2, NREP, BLK, BLK), BF),
            V((rows, BLK), BF),
            V((rows, BLK), F32),
            V((NJ, BLK, BLK), F32),
            V((NJ, MSG, NCOL * BLK), BF),
            V((NCOL, BLK, NJ * BLK), BF),
            V((NJ, MSG, BLK), F32),
            V((NJ, 1, BLK), F32),
            V((NJ, 1, BLK), F32),
            V((2, MSG, BLK), F32),
            V((NJ, 1, BLK), F32),
            V((NJ, MSG, ZH * BLK), BF),
            V((NJ, 32, BLK), BF),
            V((ZH * BLK, NJ * BLK), BF),
            V((2, NJ, MSG, BLK), BF),
            V((2, NJ, BLK, BLK), BF),
            V((2, NJ, BLK, BLK), BF),
            V((2, BLK, BLK), F32),
            V((2, OWN, BLK, BLK), BF),
            V((2, OWN, BLK, BLK), BF),
            V((2, ZH, BLK, BLK), BF),
            V((2, NJ, OTHER, BLK), BF),
            V((2, NJ, SLOT, BLK), BF),
            V((2, NJ, BLK, BLK), BF),
            V((2, NREP, BLK, BLK), BF),
            V((2, NX, BLK, BLK), F32),
            V((2, NREP, BLK, BLK), BF),
            V((NM, NY, 8, BLK), F32),
            V((NM, NY, 8, BLK), F32),
            V((NY, 8, BLK), F32),
            V((NY, 8, BLK), F32),
            V((NZ, 8, BLK), F32),
            V((NY, 8, BLK), F32),
            V((NM, NY, 8, BLK), F32),
            dma,
            *[
                dma(n)
                for n in (
                    (2, NREP), (NJ,), (2, NJ), (NJ,), (2, OWN), (2, OWN), (2, NJ), (NJ,), (2, NREP),
                )
                for _ in range(2)
            ],
            *[dma((n,)) for n in (NM, NY, NZ, NY, NM) for _ in range(2)],
        ],
        compiler_params=pltpu.CompilerParams(
            collective_id=0, has_side_effects=True, vmem_limit_bytes=56 * 1024 * 1024
        ),
    )(features, weight, cotangent, tiles.reshape(rows, BLK), source, source, target)
    return pl.pallas_call(
        _leave,
        out_shape=shapes,
        in_specs=[vmem] * 3,
        out_specs=(vmem,) * 3,
    )(*outs)


def solution(mesh):
    placed = (
        P(("rows", "rep"), None),
        P(),
        P("rows", "rep", None, None, None, None),
        P("rows", "rep", None, None),
        P("rows", "rep", None, None),
        P(("rows", "rep"), None),
    )
    return jax.shard_map(
        local,
        mesh=mesh,
        in_specs=placed,
        out_specs=(P(("rows", "rep"), None), P(), P(("rows", "rep"), None)),
        check_vma=False,
    )
```
